128 devices in a mesh: rep: 8 (over z, core), shard: 16 (over x, y).
Axes of the slice: x: 4, y: 4, z: 4, core: 2. Of those that a mesh axis runs over, the one named last changes fastest.
Arguments:
- inputs: bfloat16 [16384, 1152], P(('rep', 'shard')), may hold values from -6 to 6
- lengths: int32 [128, 2], P(('rep', 'shard')), may hold values from 1 to 64, as said below
- q_weight: bfloat16 [1152, 1024], P('shard'), may hold values from -0.1875 to 0.1875
- k_weight: bfloat16 [1152, 256], P('shard'), may hold values from -0.1875 to 0.1875
- v_weight: bfloat16 [1152, 256], P('shard'), may hold values from -0.1875 to 0.1875
- o_weight: bfloat16 [1152, 1024], P('shard'), may hold values from -0.1875 to 0.1875
- gate_weight: bfloat16 [1152, 6912], P('shard'), may hold values from -0.1875 to 0.1875
- up_weight: bfloat16 [1152, 6912], P('shard'), may hold values from -0.1875 to 0.1875
- down_weight: bfloat16 [1152, 6912], P('shard'), may hold values from -0.078125 to 0.078125
- attn_norm: bfloat16 [1152], P('shard'), may hold values from 0.5 to 1.5
- attn_post_norm: bfloat16 [1152], P('shard'), may hold values from 0.5 to 1.5
- mlp_norm: bfloat16 [1152], P('shard'), may hold values from 0.5 to 1.5
- mlp_post_norm: bfloat16 [1152], P('shard'), may hold values from 0.5 to 1.5
- query_norm: bfloat16 [256], P('shard'), may hold values from 0.5 to 1.5
- key_norm: bfloat16 [256], P('shard'), may hold values from 0.5 to 1.5
- cotangent: bfloat16 [16384, 1152], P(('rep', 'shard')), may hold values from -6 to 6
Outputs:
- outputs: bfloat16 [16384, 1152], P(('rep', 'shard'))
- input_grad: bfloat16 [16384, 1152], P(('rep', 'shard'))
- grad_q_weight: float32 [1152, 1024], P('shard')
- grad_k_weight: float32 [1152, 256], P('shard')
- grad_v_weight: float32 [1152, 256], P('shard')
- grad_o_weight: float32 [1152, 1024], P('shard')
- grad_gate_weight: float32 [1152, 6912], P('shard')
- grad_up_weight: float32 [1152, 6912], P('shard')
- grad_down_weight: float32 [1152, 6912], P('shard')
- grad_attn_norm: float32 [1152], P('shard')
- grad_attn_post_norm: float32 [1152], P('shard')
- grad_mlp_norm: float32 [1152], P('shard')
- grad_mlp_post_norm: float32 [1152], P('shard')
- grad_query_norm: float32 [256], P('shard')
- grad_key_norm: float32 [256], P('shard')
The draws below stay inside these ranges and needn't reach their ends.
Inputs may be any that keep to these rules, and one draw needn't show every extreme that they name: Each device has 2 sequence slots of 1 to 64 tokens; in every draw one device has all its lengths equal to 64, so that its 128 rows are all live.
All inputs are finite; a program needn't handle non-finite values.
Results may differ from the reference program's by a relative error of at most 0.023.
Values may be sent and summed in bfloat16 or wider, within the bound.
No kernel may reach another device: no remote copies, remote signals or barrier semaphores. Data moves between devices by JAX's collectives and lax.ppermute only.
A program may use at most 192 MiB of HBM per device.

```python
import jax
import jax.numpy as jnp
from jax import lax

D = 1152
FF = 6912
HEADS = 4
HD = 256
QW = 1024
MAXLEN = 64
SEQ_DEV = 2
TOK_DEV = 128
ROWS = 16384
DEVICES = 128


def draw_lengths(key, part):
    base = jax.random.fold_in(key, 11)
    key_dev, key_seq, key_full = jax.random.split(base, 3)
    dev_level = jax.random.randint(key_dev, (DEVICES, 1), 32, 64)
    seq_level = jax.random.randint(key_seq, (DEVICES, SEQ_DEV), 40, 64)
    drawn = 1 + dev_level * seq_level * (MAXLEN - 1) // 3969
    chosen = jax.random.randint(key_full, (), 0, DEVICES)
    device_ids = jnp.arange(DEVICES)[:, None]
    return jnp.where(device_ids == chosen, MAXLEN, drawn).astype(jnp.int32)


def levels(rng, dims, pieces, least, largest):
    level, own = 1.0, jax.random.fold_in(rng, 6)
    for dim, parts in pieces:
        steps = jnp.exp(jax.random.uniform(jax.random.fold_in(own, dim), (parts,), jnp.float32, least / len(pieces), largest / len(pieces)))
        level = level * jnp.repeat(steps, dims[dim] // parts).reshape([-1 if axis == dim else 1 for axis in range(len(dims))])
    return level


def noise(rng, extent, scale, limit, cuts=(), kind=jnp.bfloat16):
    values = jax.random.normal(rng, extent, jnp.float32) * scale
    if len(cuts) > 0:
        values = levels(rng, extent, cuts, -0.22, 0.18) * values
    return jnp.clip(values, min=-limit, max=limit).astype(kind)


def setup_inputs(seed: int = 0) -> dict:
    splits = jax.random.split(jax.random.key(seed), 17)
    return {
        "inputs": noise(splits[0], (ROWS, D), 1.0, 6.0, ((0, 128),)),
        "lengths": draw_lengths(jax.random.fold_in(splits[16], 71), 0),
        "q_weight": noise(splits[2], (D, QW), D ** -0.5, 0.1875, ((0, 16),)),
        "k_weight": noise(splits[3], (D, HD), D ** -0.5, 0.1875, ((0, 16),)),
        "v_weight": noise(splits[4], (D, HD), D ** -0.5, 0.1875, ((0, 16),)),
        "o_weight": noise(splits[5], (D, QW), QW ** -0.5, 0.1875, ((0, 16),)),
        "gate_weight": noise(splits[6], (D, FF), D ** -0.5, 0.1875, ((0, 16),)),
        "up_weight": noise(splits[7], (D, FF), D ** -0.5, 0.1875, ((0, 16),)),
        "down_weight": noise(splits[8], (D, FF), FF ** -0.5, 0.078125, ((0, 16),)),
        "attn_norm": jnp.clip(1.0 + 0.1 * jax.random.normal(splits[9], (D,), jnp.float32), 0.5, 1.5).astype(jnp.bfloat16),
        "attn_post_norm": jnp.clip(1.0 + 0.1 * jax.random.normal(splits[10], (D,), jnp.float32), 0.5, 1.5).astype(jnp.bfloat16),
        "mlp_norm": jnp.clip(1.0 + 0.1 * jax.random.normal(splits[11], (D,), jnp.float32), 0.5, 1.5).astype(jnp.bfloat16),
        "mlp_post_norm": jnp.clip(1.0 + 0.1 * jax.random.normal(splits[12], (D,), jnp.float32), 0.5, 1.5).astype(jnp.bfloat16),
        "query_norm": jnp.clip(1.0 + 0.1 * jax.random.normal(splits[13], (HD,), jnp.float32), 0.5, 1.5).astype(jnp.bfloat16),
        "key_norm": jnp.clip(1.0 + 0.1 * jax.random.normal(splits[14], (HD,), jnp.float32), 0.5, 1.5).astype(jnp.bfloat16),
        "cotangent": noise(splits[15], (ROWS, D), 1.0, 6.0, ((0, 128),)),
    }


EPSILON = 1e-06
NEGATIVE = -1e+30

def norm_scale(values, gain):
    return values * lax.rsqrt(lax.optimization_barrier(jnp.mean(values * values, axis=-1, keepdims=True)) + EPSILON) * gain

def layout(lengths, count):
    ends = jnp.cumsum(lengths).astype(jnp.int32)
    starts = (ends - lengths).astype(jnp.int32)
    row_ids = jnp.arange(count, dtype=jnp.int32)
    segment = lax.optimization_barrier(jnp.sum((row_ids[:, None] >= ends[None, :]).astype(jnp.int32), axis=1)).astype(jnp.int32)
    total = ends[-1]
    live = row_ids < total
    member = segment[:, None] == jnp.arange(lengths.shape[0], dtype=jnp.int32)[None, :]
    begin = lax.optimization_barrier(jnp.sum(jnp.where(member, starts[None, :], 0), axis=1)).astype(jnp.int32)
    begin = begin + jnp.where(live, 0, total).astype(jnp.int32)
    return (segment, live, (row_ids - begin).astype(jnp.int32), row_ids)

def rotary_tables(position, width):
    half = width // 2
    freqs = 10000.0 ** (-2.0 * jnp.arange(half, dtype=jnp.float32) / width)
    angle = position.astype(jnp.float32)[:, None] * freqs[None, :]
    return (jnp.cos(angle), jnp.sin(angle))

def head_prep(values, gain, cosine, sine):
    normed = norm_scale(values, gain)
    half = values.shape[-1] // 2
    first = normed[..., :half]
    second = normed[..., half:]
    cos_b = cosine[:, None, :]
    sin_b = sine[:, None, :]
    return jnp.concatenate([first * cos_b - second * sin_b, second * cos_b + first * sin_b], axis=-1)

def geglu(gate, up):
    return jax.nn.gelu(gate, approximate=True) * up

def layer_block(block_in, block_len, block_cot, weights, gains):
    q_weight, k_weight, v_weight, o_weight, gate_weight, up_weight, down_weight = weights
    gain_attn, gain_post, gain_mid, gain_last, gain_query, gain_key = gains
    count = block_in.shape[0]
    segment, live, position, row_ids = layout(block_len, count)
    live_col = live.astype(jnp.float32)[:, None]
    cosine, sine = rotary_tables(position, HD)
    same = (segment[:, None] == segment[None, :]) & (row_ids[None, :] <= row_ids[:, None])
    scale = HD ** (-0.5)
    residual = block_in.astype(jnp.float32)
    normed_one = norm_scale(residual, gain_attn).astype(jnp.bfloat16)
    query_acc = jnp.dot(normed_one, q_weight, preferred_element_type=jnp.float32)
    key_acc = jnp.dot(normed_one, k_weight, preferred_element_type=jnp.float32)
    value_b = jnp.dot(normed_one, v_weight, preferred_element_type=jnp.float32).astype(jnp.bfloat16)
    query_heads = query_acc.reshape(count, HEADS, HD)
    key_heads = key_acc.reshape(count, 1, HD)
    query_rot = head_prep(query_heads, gain_query, cosine, sine).astype(jnp.bfloat16)
    key_rot = head_prep(key_heads, gain_key, cosine, sine)[:, 0].astype(jnp.bfloat16)
    scores = jnp.einsum('qhd,kd->hqk', query_rot.astype(jnp.float32), key_rot.astype(jnp.float32)) * scale
    scores = jnp.where(same[None], scores, NEGATIVE)
    peak = lax.optimization_barrier(jnp.max(scores, axis=-1, keepdims=True))
    log_total = peak + jnp.log(lax.optimization_barrier(jnp.sum(jnp.exp(scores - peak), axis=-1, keepdims=True)))
    probs = jnp.exp(scores - log_total)
    probs_b = probs.astype(jnp.bfloat16)
    mixed = jnp.einsum('hqk,kd->qhd', probs_b.astype(jnp.float32), value_b.astype(jnp.float32))
    mixed = mixed.reshape(count, HEADS * HD).astype(jnp.bfloat16)
    attention = jnp.dot(mixed, o_weight.T, preferred_element_type=jnp.float32)
    middle = residual + norm_scale(attention, gain_post)
    normed_two = norm_scale(middle, gain_mid).astype(jnp.bfloat16)
    gate_acc = jnp.dot(normed_two, gate_weight, preferred_element_type=jnp.float32)
    up_acc = jnp.dot(normed_two, up_weight, preferred_element_type=jnp.float32)
    hidden_b = geglu(gate_acc, up_acc).astype(jnp.bfloat16)
    feed = jnp.dot(hidden_b, down_weight.T, preferred_element_type=jnp.float32)
    outputs = ((middle + norm_scale(feed, gain_last)) * live_col).astype(jnp.bfloat16)
    grad_out = block_cot.astype(jnp.float32) * live_col
    unused, pull_last = jax.vjp(norm_scale, feed, gain_last)
    grad_feed, grad_last = pull_last(grad_out)
    feed_b = grad_feed.astype(jnp.bfloat16)
    grad_down = jnp.dot(feed_b.T, hidden_b, preferred_element_type=jnp.float32)
    grad_hidden = jnp.dot(feed_b, down_weight, preferred_element_type=jnp.float32)
    unused, pull_glu = jax.vjp(geglu, gate_acc, up_acc)
    grad_gate, grad_up = pull_glu(grad_hidden)
    gate_b = grad_gate.astype(jnp.bfloat16)
    up_b = grad_up.astype(jnp.bfloat16)
    grad_gate_w = jnp.dot(normed_two.T, gate_b, preferred_element_type=jnp.float32)
    grad_up_w = jnp.dot(normed_two.T, up_b, preferred_element_type=jnp.float32)
    grad_normed = jnp.dot(gate_b, gate_weight.T, preferred_element_type=jnp.float32)
    grad_normed = grad_normed + jnp.dot(up_b, up_weight.T, preferred_element_type=jnp.float32)
    unused, pull_mid = jax.vjp(norm_scale, middle, gain_mid)
    back_mid, grad_mid = pull_mid(grad_normed)
    grad_middle = grad_out + back_mid
    unused, pull_post = jax.vjp(norm_scale, attention, gain_post)
    grad_attention, grad_post = pull_post(grad_middle)
    attention_b = grad_attention.astype(jnp.bfloat16)
    grad_o = jnp.dot(attention_b.T, mixed, preferred_element_type=jnp.float32)
    grad_mixed = jnp.dot(attention_b, o_weight, preferred_element_type=jnp.float32).astype(jnp.bfloat16)
    grad_mixed = grad_mixed.reshape(count, HEADS, HD).astype(jnp.float32)
    grad_probs = jnp.einsum('qhd,kd->hqk', grad_mixed, value_b.astype(jnp.float32))
    inner = lax.optimization_barrier(jnp.sum(probs * grad_probs, axis=-1, keepdims=True))
    grad_scores = (probs * (grad_probs - inner) * scale).astype(jnp.bfloat16).astype(jnp.float32)
    grad_qrot = jnp.einsum('hqk,kd->qhd', grad_scores, key_rot.astype(jnp.float32))
    grad_krot = jnp.einsum('hqk,qhd->kd', grad_scores, query_rot.astype(jnp.float32))
    grad_value = jnp.einsum('hqk,qhd->kd', probs_b.astype(jnp.float32), grad_mixed)
    unused, pull_query = jax.vjp(lambda values, gain: head_prep(values, gain, cosine, sine), query_heads, gain_query)
    grad_query, grad_qgain = pull_query(grad_qrot)
    unused, pull_key = jax.vjp(lambda values, gain: head_prep(values, gain, cosine, sine), key_heads, gain_key)
    grad_key, grad_kgain = pull_key(grad_krot[:, None, :])
    query_b = grad_query.reshape(count, HEADS * HD).astype(jnp.bfloat16)
    key_b = grad_key.reshape(count, HD).astype(jnp.bfloat16)
    value_grad_b = grad_value.astype(jnp.bfloat16)
    grad_q = jnp.dot(normed_one.T, query_b, preferred_element_type=jnp.float32)
    grad_k = jnp.dot(normed_one.T, key_b, preferred_element_type=jnp.float32)
    grad_v = jnp.dot(normed_one.T, value_grad_b, preferred_element_type=jnp.float32)
    grad_first_in = jnp.dot(query_b, q_weight.T, preferred_element_type=jnp.float32)
    grad_first_in = grad_first_in + jnp.dot(key_b, k_weight.T, preferred_element_type=jnp.float32)
    grad_first_in = grad_first_in + jnp.dot(value_grad_b, v_weight.T, preferred_element_type=jnp.float32)
    unused, pull_first = jax.vjp(norm_scale, residual, gain_attn)
    back_first, grad_first = pull_first(grad_first_in)
    input_grad = (grad_middle + back_first).astype(jnp.bfloat16)
    grads = (grad_q, grad_k, grad_v, grad_o, grad_gate_w, grad_up_w, grad_down, grad_first, grad_post, grad_mid, grad_last, grad_qgain, grad_kgain)
    return (outputs, input_grad, grads)

def reference(inputs, lengths, q_weight, k_weight, v_weight, o_weight, gate_weight, up_weight, down_weight, attn_norm, attn_post_norm, mlp_norm, mlp_post_norm, query_norm, key_norm, cotangent):
    weights = (q_weight, k_weight, v_weight, o_weight, gate_weight, up_weight, down_weight)
    gains = (attn_norm.astype(jnp.float32), attn_post_norm.astype(jnp.float32), mlp_norm.astype(jnp.float32), mlp_post_norm.astype(jnp.float32), query_norm.astype(jnp.float32), key_norm.astype(jnp.float32))
    shapes = [(D, HEADS * HD), (D, HD), (D, HD), (D, HEADS * HD), (D, FF), (D, FF), (D, FF), (D,), (D,), (D,), (D,), (HD,), (HD,)]
    start_grads = tuple((jnp.zeros(shape, jnp.float32) for shape in shapes))
    blocks = (inputs.reshape(DEVICES, TOK_DEV, D), lengths, cotangent.reshape(DEVICES, TOK_DEV, D))

    def step(carry, block):
        outputs, input_grad, grads = layer_block(block[0], block[1], block[2], weights, gains)
        return (tuple((old + new for old, new in zip(carry, grads))), (outputs, input_grad))
    totals, produced = lax.scan(step, start_grads, blocks)
    return (produced[0].reshape(ROWS, D), produced[1].reshape(ROWS, D), totals[0], totals[1], totals[2], totals[3], totals[4], totals[5], totals[6], totals[7], totals[8], totals[9], totals[10], totals[11], totals[12])
```

```python
import jax
import jax.numpy as jnp
from jax import lax
from jax.sharding import PartitionSpec as P

EPSILON = 1e-06
NEGATIVE = -1e30
BF = jnp.bfloat16
F32 = jnp.float32


def norm_scale(values, gain):
    return values * lax.rsqrt(jnp.mean(values * values, axis=-1, keepdims=True) + EPSILON) * gain


def unit_rows(values):
    return values * lax.rsqrt(jnp.mean(values * values, axis=-1, keepdims=True) + EPSILON)


def layout(lengths, count):
    ends = jnp.cumsum(lengths)
    starts = ends - lengths
    row_ids = jnp.arange(count, dtype=jnp.int32)
    segment = jnp.sum((row_ids[:, None] >= ends[None, :]).astype(jnp.int32), axis=1)
    total = ends[-1]
    live = row_ids < total
    member = segment[:, None] == jnp.arange(lengths.shape[0], dtype=jnp.int32)[None, :]
    begin = jnp.sum(jnp.where(member, starts[None, :], 0), axis=1)
    begin = begin + jnp.where(live, 0, total)
    return (segment, live, row_ids - begin, row_ids)


def rotary_tables(position, width):
    half = width // 2
    freqs = 10000.0 ** (-2.0 * jnp.arange(half, dtype=jnp.float32) / width)
    angle = position.astype(jnp.float32)[:, None] * freqs[None, :]
    return (jnp.cos(angle), jnp.sin(angle))


def head_prep(values, gain, cosine, sine):
    normed = norm_scale(values, gain)
    half = values.shape[-1] // 2
    first = normed[..., :half]
    second = normed[..., half:]
    cos_b = cosine[:, None, :]
    sin_b = sine[:, None, :]
    return jnp.concatenate(
        [first * cos_b - second * sin_b, second * cos_b + first * sin_b], axis=-1
    )


def geglu(gate, up):
    return jax.nn.gelu(gate, approximate=True) * up


def dot_rows(left, right):
    return lax.dot_general(
        left, right, (((1,), (1,)), ((), ())), preferred_element_type=jnp.float32
    )


def dot_cols(left, right):
    return lax.dot_general(
        left, right, (((0,), (0,)), ((), ())), preferred_element_type=jnp.float32
    )


def z_perm(d):
    return [(i, ((i // 2 + d) % 4) * 2 + i % 2) for i in range(8)]


CORE_PERM = [(i, i ^ 1) for i in range(8)]


def x_perm(d):
    return [(i, ((i // 4 + d) % 4) * 4 + i % 4) for i in range(16)]


def y_perm(d):
    return [(i, (i // 4) * 4 + (i % 4 + d) % 4) for i in range(16)]


def shift_z(v, d):
    return lax.ppermute(v, "rep", z_perm(d % 4))


def swap_core(v):
    return lax.ppermute(v, "rep", CORE_PERM)


def shift_xy(v, axis, d):
    return lax.ppermute(v, "shard", x_perm(d % 4) if axis == "x" else y_perm(d % 4))


def pick(stack, index):
    return lax.dynamic_index_in_dim(stack, index, 0, keepdims=False)


def ring_gather(own, axis, index):
    cut = (own.shape[0] + 1) // 2 if own.ndim == 3 else (own.shape[0] // 16) * 8
    after = shift_xy(own, axis, 3)
    before = shift_xy(own, axis, 1)
    far_a = shift_xy(before[:cut], axis, 1)
    far_b = shift_xy(after[cut:], axis, 3)
    far = jnp.concatenate([far_a, far_b], axis=0)
    ring = jnp.stack([own, after, far, before, own, after, far, before])
    return lax.dynamic_slice_in_dim(ring, (4 - index) % 4, 4, 0)


def ring_reduce(groups, axis, index):
    own, after, far, before = [pick(groups, (index + e) % 4) for e in range(4)]
    cut = (own.shape[0] + 1) // 2 if own.ndim == 3 else (own.shape[0] // 16) * 8
    got_a = shift_xy(far[:cut], axis, 1)
    got_b = shift_xy(far[cut:], axis, 3)
    to_after = jnp.concatenate([after[:cut] + got_a, after[cut:]], axis=0)
    to_before = jnp.concatenate([before[:cut], before[cut:] + got_b], axis=0)
    from_before = shift_xy(to_after, axis, 1)
    from_after = shift_xy(to_before, axis, 3)
    total = own.astype(F32) + from_before.astype(F32) + from_after.astype(F32)
    return total.astype(BF)


def gather_xy(block, xi, yi, cut):
    rows = block.shape[0]
    one, two = block[:, :cut], block[:, cut:]
    one = ring_gather(ring_gather(one, "x", xi), "y", yi)
    two = ring_gather(ring_gather(two, "y", yi), "x", xi)
    one = jnp.transpose(one, (1, 0, 2, 3)).reshape(16, rows, cut)
    two = two.reshape(16, rows, block.shape[1] - cut)
    return jnp.concatenate([one, two], axis=2)


def reduce_xy(full, xi, yi, cut):
    rows, width = full.shape[1], full.shape[2]
    parts = full.reshape(4, 4, rows, width)
    one = jnp.transpose(parts[..., :cut], (1, 0, 2, 3))
    two = parts[..., cut:]
    one = ring_reduce(ring_reduce(one, "y", yi), "x", xi)
    two = ring_reduce(ring_reduce(two, "x", xi), "y", yi)
    return jnp.concatenate([one, two], axis=1)


def gather_rep(v):
    mine = jnp.concatenate([v, shift_z(v, 1), shift_z(v, 2), shift_z(v, 3)], axis=0)
    return jnp.concatenate([mine, swap_core(mine)], axis=0)


def reduce_rep(part):
    rows = part.shape[0] // 2
    got = swap_core(part[rows:].astype(BF))
    total = part[:rows] + got.astype(F32)
    count = rows // 4
    send = [total[j * count : (j + 1) * count].astype(BF) for j in range(1, 4)]
    moved = [shift_z(send[j - 1], 4 - j) for j in range(1, 4)]
    out = total[:count]
    for m in moved:
        out = out + m.astype(F32)
    return out


def rep_order(own, zi, core):
    before = [own] + [shift_z(own, d) for d in (1, 2, 3)]
    mine = jnp.stack([before[0], before[3], before[2], before[1]])
    other = swap_core(mine)
    first = core == 0
    pair = jnp.stack([jnp.where(first, mine, other), jnp.where(first, other, mine)], axis=1)
    pair = jnp.concatenate([pair, pair], axis=0)
    pair = lax.dynamic_slice_in_dim(pair, (4 - zi) % 4, 4, 0)
    return pair.reshape((8,) + own.shape)


USE_XLA_BULK = False


def per_device(
    inputs,
    lengths,
    q_weight,
    k_weight,
    v_weight,
    o_weight,
    gate_weight,
    up_weight,
    down_weight,
    attn_norm,
    attn_post_norm,
    mlp_norm,
    mlp_post_norm,
    query_norm,
    key_norm,
    cotangent,
):
    count, model = inputs.shape
    local = q_weight.shape[0]
    head_local = query_norm.shape[0]
    head_width = 16 * head_local
    q_width = q_weight.shape[1]
    ff_width = gate_weight.shape[1]
    heads = q_width // head_width
    scale = head_width ** (-0.5)
    rep = lax.axis_index("rep")
    shard = lax.axis_index("shard")
    zi, core = rep // 2, rep % 2
    xi, yi = shard // 4, shard % 4

    gains = jnp.concatenate(
        [attn_norm, attn_post_norm, mlp_norm, mlp_post_norm, query_norm, key_norm]
    )
    half_width = q_width + head_width
    low = jnp.concatenate([q_weight, k_weight], axis=1)
    high = jnp.concatenate([v_weight, o_weight], axis=1)
    half_w = jnp.where(core == 0, low, high)
    gain_rows = jnp.pad(gains[None, :], ((0, 7), (0, half_width - gains.shape[0])))
    half_w = jnp.concatenate([half_w, gain_rows], axis=0)
    got = gather_xy(half_w, xi, yi, 640)
    all_gains = got[:, local, : gains.shape[0]].astype(F32)
    got_w = got[:, :local, :].reshape(model, half_width)
    peer_w = swap_core(got_w)
    full_low = jnp.where(core == 0, got_w, peer_w)
    full_high = jnp.where(core == 0, peer_w, got_w)
    full_q, full_k = full_low[:, :q_width], full_low[:, q_width:]
    full_v, full_o = full_high[:, :head_width], full_high[:, head_width:]
    gain_attn = all_gains[:, :local].reshape(model)
    gain_post = all_gains[:, local : 2 * local].reshape(model)
    gain_mid = all_gains[:, 2 * local : 3 * local].reshape(model)
    gain_last = all_gains[:, 3 * local : 4 * local].reshape(model)
    gain_query = all_gains[:, 4 * local : 4 * local + head_local].reshape(head_width)
    gain_key = all_gains[:, 4 * local + head_local :].reshape(head_width)

    unit = 7 * (ff_width // 54)
    first_unit = jnp.minimum(rep * unit, ff_width - unit)
    valid = (first_unit + jnp.arange(unit, dtype=jnp.int32) >= rep * unit)[None, :]
    mine_w = jnp.concatenate(
        [
            lax.dynamic_slice_in_dim(w, first_unit, unit, 1)
            for w in (gate_weight, up_weight, down_weight)
        ],
        axis=1,
    )
    if USE_XLA_BULK:
        ff_w = lax.all_gather(mine_w, "shard", axis=0, tiled=True)
    else:
        ff_w = gather_xy(mine_w, xi, yi, 1280).reshape(model, 3 * unit)
    w_gate, w_up, w_down = ff_w[:, :unit], ff_w[:, unit : 2 * unit], ff_w[:, 2 * unit :]

    segment, live, position, row_ids = layout(lengths[0], count)
    live_col = live.astype(jnp.float32)[:, None]
    cosine, sine = rotary_tables(position, head_width)
    same = (segment[:, None] == segment[None, :]) & (row_ids[None, :] <= row_ids[:, None])
    residual = inputs.astype(jnp.float32)
    normed_one = norm_scale(residual, gain_attn).astype(BF)
    query_acc = jnp.dot(normed_one, full_q, preferred_element_type=F32)
    key_acc = jnp.dot(normed_one, full_k, preferred_element_type=F32)
    value_b = jnp.dot(normed_one, full_v, preferred_element_type=F32).astype(BF)
    query_heads = query_acc.reshape(count, heads, head_width)
    key_heads = key_acc.reshape(count, 1, head_width)
    query_rot = head_prep(query_heads, gain_query, cosine, sine).astype(BF)
    key_rot = head_prep(key_heads, gain_key, cosine, sine)[:, 0].astype(BF)

    raw = jnp.einsum("qhd,kd->hqk", query_rot, key_rot, preferred_element_type=F32) * scale
    scores = jnp.where(same[None], raw, NEGATIVE)
    peak = jnp.max(scores, axis=-1, keepdims=True)
    log_total = peak + jnp.log(jnp.sum(jnp.exp(scores - peak), axis=-1, keepdims=True))
    probs = jnp.exp(scores - log_total)
    probs_b = probs.astype(BF)
    mixed = jnp.einsum("hqk,kd->qhd", probs_b, value_b, preferred_element_type=F32)
    mixed = mixed.reshape(count, q_width).astype(BF)
    attention = dot_rows(mixed, full_o)
    middle = residual + norm_scale(attention, gain_post)
    normed_two = norm_scale(middle, gain_mid).astype(BF)

    rows_two = gather_rep(normed_two)
    gate_acc = jnp.dot(rows_two, w_gate, preferred_element_type=F32)
    up_acc = jnp.dot(rows_two, w_up, preferred_element_type=F32)
    hidden_b = jnp.where(valid, geglu(gate_acc, up_acc), 0.0).astype(BF)
    feed = reduce_rep(dot_rows(hidden_b, w_down))
    outputs = ((middle + norm_scale(feed, gain_last)) * live_col).astype(BF)

    grad_out = cotangent.astype(jnp.float32) * live_col
    unused, pull_last = jax.vjp(norm_scale, feed, gain_last)
    grad_feed, grad_last = pull_last(grad_out)
    rows_feed = gather_rep(grad_feed.astype(BF))
    grad_hidden = jnp.dot(rows_feed, w_down, preferred_element_type=F32)
    unused, pull_glu = jax.vjp(geglu, gate_acc, up_acc)
    grad_gate, grad_up = pull_glu(jnp.where(valid, grad_hidden, 0.0))
    gate_b = grad_gate.astype(BF)
    up_b = grad_up.astype(BF)
    grad_normed = reduce_rep(dot_rows(gate_b, w_gate) + dot_rows(up_b, w_up))

    ff_grads = jnp.concatenate(
        [
            dot_cols(rows_two, gate_b).astype(BF),
            dot_cols(rows_two, up_b).astype(BF),
            dot_cols(rows_feed, hidden_b).astype(BF),
        ],
        axis=1,
    )
    if USE_XLA_BULK:
        ff_sum = lax.psum_scatter(ff_grads, "shard", scatter_dimension=0, tiled=True)
    else:
        ff_sum = reduce_xy(ff_grads.reshape(16, local, 3 * unit), xi, yi, 1280)
    ff_all = rep_order(ff_sum, zi, core)

    unused, pull_mid = jax.vjp(norm_scale, middle, gain_mid)
    back_mid, grad_mid = pull_mid(grad_normed)
    grad_middle = grad_out + back_mid
    unused, pull_post = jax.vjp(norm_scale, attention, gain_post)
    grad_attention, grad_post = pull_post(grad_middle)
    attention_b = grad_attention.astype(BF)
    grad_mixed = jnp.dot(attention_b, full_o, preferred_element_type=F32).astype(BF)
    grad_mixed = grad_mixed.reshape(count, heads, head_width)
    grad_probs = jnp.einsum("qhd,kd->hqk", grad_mixed, value_b, preferred_element_type=F32)
    inner = jnp.sum(probs * grad_probs, axis=-1, keepdims=True)
    grad_scores = (probs * (grad_probs - inner) * scale).astype(BF)
    grad_qrot = jnp.einsum("hqk,kd->qhd", grad_scores, key_rot, preferred_element_type=F32)
    grad_krot = jnp.einsum("hqk,qhd->kd", grad_scores, query_rot, preferred_element_type=F32)
    grad_value = jnp.einsum("hqk,qhd->kd", probs_b, grad_mixed, preferred_element_type=F32)
    unused, pull_query = jax.vjp(
        lambda values, gain: head_prep(values, gain, cosine, sine), query_heads, gain_query
    )
    grad_query, grad_qgain = pull_query(grad_qrot)
    unused, pull_key = jax.vjp(
        lambda values, gain: head_prep(values, gain, cosine, sine), key_heads, gain_key
    )
    grad_key, grad_kgain = pull_key(grad_krot[:, None, :])
    query_b = grad_query.reshape(count, q_width).astype(BF)
    key_b = grad_key.reshape(count, head_width).astype(BF)
    value_grad_b = grad_value.astype(BF)
    grad_first_in = (
        dot_rows(query_b, full_q) + dot_rows(key_b, full_k) + dot_rows(value_grad_b, full_v)
    )
    unused, pull_first = jax.vjp(norm_scale, residual, gain_attn)
    back_first, grad_first = pull_first(grad_first_in)
    input_grad = (grad_middle + back_first).astype(BF)

    grad_low = dot_cols(normed_one, jnp.concatenate([query_b, key_b], axis=1)).astype(BF)
    grad_high = jnp.concatenate(
        [dot_cols(normed_one, value_grad_b).astype(BF), dot_cols(attention_b, mixed).astype(BF)],
        axis=1,
    )
    gain_grads = jnp.concatenate(
        [
            g.reshape(16, 1, -1)
            for g in (grad_first, grad_post, grad_mid, grad_last, grad_qgain, grad_kgain)
        ],
        axis=2,
    )
    gain_grads = jnp.pad(
        gain_grads, ((0, 0), (0, 7), (0, half_width - gain_grads.shape[2]))
    ).astype(BF)
    keep = jnp.where(core == 0, grad_low, grad_high)
    give = jnp.where(core == 0, grad_high, grad_low)
    keep = jnp.concatenate([keep.reshape(16, local, half_width), gain_grads], axis=1)
    give = jnp.concatenate([give.reshape(16, local, half_width), gain_grads], axis=1)
    pair_sum = (keep.astype(F32) + swap_core(give).astype(F32)).astype(BF)
    part = reduce_xy(pair_sum, xi, yi, 640)
    total = part.astype(F32)
    for d in (1, 2, 3):
        total = total + shift_z(part, d).astype(F32)
    peer = swap_core(total.astype(BF)).astype(F32)
    low_total = jnp.where(core == 0, total, peer)
    high_total = jnp.where(core == 0, peer, total)
    gain_total = low_total[local, :]

    pieces = []
    for m in range(3):
        cols = [ff_all[r, :, m * unit : (m + 1) * unit] for r in range(8)]
        cols[7] = cols[7][:, 8 * unit - ff_width :]
        pieces.append(jnp.concatenate(cols, axis=1).astype(F32))
    return (
        outputs,
        input_grad,
        low_total[:local, :q_width],
        low_total[:local, q_width:],
        high_total[:local, :head_width],
        high_total[:local, head_width:],
        pieces[0],
        pieces[1],
        pieces[2],
        gain_total[:local],
        gain_total[local : 2 * local],
        gain_total[2 * local : 3 * local],
        gain_total[3 * local : 4 * local],
        gain_total[4 * local : 4 * local + head_local],
        gain_total[4 * local + head_local : 4 * local + 2 * head_local],
    )


def solution(mesh):
    tokens, rows, vector = P(("rep", "shard"), None), P("shard", None), P("shard")
    in_specs = (tokens, tokens) + (rows,) * 7 + (vector,) * 6 + (tokens,)
    out_specs = (tokens, tokens) + (rows,) * 7 + (vector,) * 6
    return jax.shard_map(
        per_device, mesh=mesh, in_specs=in_specs, out_specs=out_specs, check_vma=False
    )
```

```python
import math

import jax
import jax.numpy as jnp
from jax import lax
from jax.experimental import pallas as pl
from jax.experimental.pallas import tpu as pltpu
from jax.sharding import PartitionSpec as P

EPSILON = 1e-06
NEGATIVE = -1e30
BF = jnp.bfloat16
F32 = jnp.float32


def norm_scale(values, gain):
    return values * lax.rsqrt(jnp.mean(values * values, axis=-1, keepdims=True) + EPSILON) * gain


def unit_rows(values):
    return values * lax.rsqrt(jnp.mean(values * values, axis=-1, keepdims=True) + EPSILON)


def layout(lengths, count):
    ends = jnp.cumsum(lengths)
    starts = ends - lengths
    row_ids = jnp.arange(count, dtype=jnp.int32)
    segment = jnp.sum((row_ids[:, None] >= ends[None, :]).astype(jnp.int32), axis=1)
    total = ends[-1]
    live = row_ids < total
    member = segment[:, None] == jnp.arange(lengths.shape[0], dtype=jnp.int32)[None, :]
    begin = jnp.sum(jnp.where(member, starts[None, :], 0), axis=1)
    begin = begin + jnp.where(live, 0, total)
    return (segment, live, row_ids - begin, row_ids)


def rotary_tables(position, width):
    half = width // 2
    freqs = 10000.0 ** (-2.0 * jnp.arange(half, dtype=jnp.float32) / width)
    angle = position.astype(jnp.float32)[:, None] * freqs[None, :]
    return (jnp.cos(angle), jnp.sin(angle))


def head_prep(values, gain, cosine, sine):
    normed = norm_scale(values, gain)
    half = values.shape[-1] // 2
    first = normed[..., :half]
    second = normed[..., half:]
    cos_b = cosine[:, None, :]
    sin_b = sine[:, None, :]
    return jnp.concatenate(
        [first * cos_b - second * sin_b, second * cos_b + first * sin_b], axis=-1
    )


def geglu(gate, up):
    return jax.nn.gelu(gate, approximate=True) * up


FF_UNIT = 896


def dot_rows(left, right):
    return lax.dot_general(
        left, right, (((1,), (1,)), ((), ())), preferred_element_type=jnp.float32
    )


def dot_cols(left, right):
    return lax.dot_general(
        left, right, (((0,), (0,)), ((), ())), preferred_element_type=jnp.float32
    )


def z_perm(d):
    return [(i, ((i // 2 + d) % 4) * 2 + i % 2) for i in range(8)]


CORE_PERM = [(i, i ^ 1) for i in range(8)]


def x_perm(d):
    return [(i, ((i // 4 + d) % 4) * 4 + i % 4) for i in range(16)]


def y_perm(d):
    return [(i, (i // 4) * 4 + (i % 4 + d) % 4) for i in range(16)]


def shift(v, axis, d):
    if axis == "z":
        return lax.ppermute(v, "rep", z_perm(d % 4))
    return lax.ppermute(v, "shard", x_perm(d % 4) if axis == "x" else y_perm(d % 4))


def swap_core(v):
    return lax.ppermute(v, "rep", CORE_PERM)


def direct_gather(own, axis):
    return [own] + [shift(own, axis, -e) for e in (1, 2, 3)]


def direct_reduce(groups, axis):
    total = groups[0].astype(F32)
    for e in (1, 2, 3):
        total = total + shift(groups[e], axis, e).astype(F32)
    return total


def pick(stack, index, axis, e):
    return lax.dynamic_index_in_dim(stack, (index + e) % 4, axis, keepdims=False)


def split_xy(one, two, xi, yi):
    rows = one.shape[0] // 16
    one = one.reshape(4, 4, rows, -1)
    two = two.reshape(4, 4, rows, -1)
    return [pick(one, yi, 1, e) for e in range(4)], [pick(two, xi, 0, e) for e in range(4)]


def finish_xy(one, two, xi, yi):
    one, two = one.astype(BF), two.astype(BF)
    one = direct_reduce([pick(one, xi, 0, e) for e in range(4)], "x")
    two = direct_reduce([pick(two, yi, 0, e) for e in range(4)], "y")
    return one, two


def place_xy(pieces, info, x_inside, split):
    rows, width = pieces[0].shape[1:]

    def body(info_ref, *refs):
        low_ref, high_ref = refs[4:]
        for e in range(4):
            for f in range(4):
                dx, dy = (f, e) if x_inside else (e, f)
                x = lax.rem(info_ref[3] + dx, 4)
                y = lax.rem(info_ref[4] + dy, 4)
                low_ref[x * 4 + y] = refs[e][f, :, :split]
                high_ref[x * 4 + y] = refs[e][f, :, split:]

    vmem = pl.BlockSpec(memory_space=pltpu.VMEM)
    low, high = pl.pallas_call(
        body,
        in_specs=[pl.BlockSpec(memory_space=pltpu.SMEM)] + [vmem] * 4,
        out_specs=[vmem, vmem],
        out_shape=[
            jax.ShapeDtypeStruct((16, rows, split), BF),
            jax.ShapeDtypeStruct((16, rows, width - split), BF),
        ],
        cost_estimate=pl.CostEstimate(flops=0, bytes_accessed=4_000_000, transcendentals=0),
        name="place_xy",
    )(info, *pieces)
    return low.reshape(16 * rows, split), high.reshape(16 * rows, width - split)


def gather_rep(v):
    mine = jnp.concatenate(direct_gather(v, "z"), axis=0)
    return swap_core(mine), mine


def reduce_rep(other, mine):
    total = mine + swap_core(other).astype(F32)
    count = total.shape[0] // 4
    sends = total[count:].astype(BF)
    out = total[:count]
    for e in (1, 2, 3):
        out = out + shift(sends[(e - 1) * count : e * count], "z", e).astype(F32)
    return out


TILE = 256
CHUNKS = ((0, 896),)
NT = (((1,), (1,)), ((), ()))
TN = (((0,), (0,)), ((), ()))


def mm(left, right, dims=(((1,), (0,)), ((), ()))):
    return lax.dot_general(left, right, dims, preferred_element_type=F32)


def row_specs(width, steps):
    half = steps // 2
    return [
        pl.BlockSpec((TILE, width), lambda i: (jnp.minimum(i, half - 1), 0)),
        pl.BlockSpec((TILE, width), lambda i: (jnp.maximum(i - half, 0), 0)),
    ]


def put_rows(step, half, value, other_ref, mine_ref):
    @pl.when(step < half)
    def _():
        other_ref[...] = value.astype(other_ref.dtype)

    @pl.when(step >= half)
    def _():
        mine_ref[...] = value.astype(mine_ref.dtype)


def ff_forward(other, mine, weights, info):
    steps = 2 * other.shape[0] // TILE
    model, unit = other.shape[1], FF_UNIT
    half = steps // 2

    def body(info_ref, o_ref, m_ref, w_ref, hid_ref, act_ref, der_ref, fo_ref, fm_ref):
        step = pl.program_id(0)
        x = jnp.where(step < half, o_ref[...], m_ref[...])
        feed = 0.0
        c = math.sqrt(2.0 / math.pi)
        for lo, hi in CHUNKS:
            gate = mm(x, w_ref[:, lo:hi])
            up = mm(x, w_ref[:, unit + lo : unit + hi])
            col = lo + lax.broadcasted_iota(jnp.int32, gate.shape, 1)
            valid = col >= info_ref[0]
            square = gate * gate
            t = jnp.tanh(c * (gate + 0.044715 * (gate * square)))
            act = jnp.where(valid, 0.5 * gate * (1.0 + t), 0.0)
            slope = 0.5 * (1.0 + t) + 0.5 * gate * (1.0 - t * t) * (
                c + (3 * 0.044715 * c) * square
            )
            hid = (act * up).astype(BF)
            hid_ref[:, lo:hi] = hid
            act_ref[:, lo:hi] = act.astype(BF)
            der_ref[:, lo:hi] = jnp.where(valid, slope * up, 0.0).astype(BF)
            feed = feed + mm(hid, w_ref[:, 2 * unit + lo : 2 * unit + hi], NT)
        put_rows(step, half, feed, fo_ref, fm_ref)

    whole = lambda w: pl.BlockSpec(w.shape, lambda i: (0, 0))
    wide = pl.BlockSpec((TILE, unit), lambda i: (i, 0))
    rows = other.shape[0]
    return pl.pallas_call(
        body,
        grid=(steps,),
        in_specs=[pl.BlockSpec(memory_space=pltpu.SMEM)]
        + row_specs(model, steps)
        + [whole(weights)],
        out_specs=[wide, wide, wide] + row_specs(model, steps),
        out_shape=[jax.ShapeDtypeStruct((2 * rows, unit), BF)] * 3
        + [jax.ShapeDtypeStruct((rows, model), BF), jax.ShapeDtypeStruct((rows, model), F32)],
        cost_estimate=pl.CostEstimate(
            flops=12 * rows * model * unit, bytes_accessed=20_000_000, transcendentals=0
        ),
        name="ff_forward",
    )(info, other, mine, weights)


def ff_backward(other, mine, act, der, weights):
    steps = 2 * other.shape[0] // TILE
    model, unit = other.shape[1], FF_UNIT
    half = steps // 2

    def body(o_ref, m_ref, act_ref, der_ref, w_ref, gg_ref, gu_ref, bo_ref, bm_ref):
        step = pl.program_id(0)
        x = jnp.where(step < half, o_ref[...], m_ref[...])
        back = 0.0
        for lo, hi in CHUNKS:
            ghid = mm(x, w_ref[:, 2 * unit + lo : 2 * unit + hi])
            ggate = (ghid * der_ref[:, lo:hi].astype(F32)).astype(BF)
            gup = (ghid * act_ref[:, lo:hi].astype(F32)).astype(BF)
            gg_ref[:, lo:hi] = ggate
            gu_ref[:, lo:hi] = gup
            back = back + mm(ggate, w_ref[:, lo:hi], NT)
            back = back + mm(gup, w_ref[:, unit + lo : unit + hi], NT)
        put_rows(step, half, back, bo_ref, bm_ref)

    whole = lambda w: pl.BlockSpec(w.shape, lambda i: (0, 0))
    wide = pl.BlockSpec((TILE, unit), lambda i: (i, 0))
    rows = other.shape[0]
    return pl.pallas_call(
        body,
        grid=(steps,),
        in_specs=row_specs(model, steps) + [wide, wide, whole(weights)],
        out_specs=[wide, wide] + row_specs(model, steps),
        out_shape=[jax.ShapeDtypeStruct((2 * rows, unit), BF)] * 2
        + [jax.ShapeDtypeStruct((rows, model), BF), jax.ShapeDtypeStruct((rows, model), F32)],
        cost_estimate=pl.CostEstimate(
            flops=12 * rows * model * unit, bytes_accessed=20_000_000, transcendentals=0
        ),
        name="ff_backward",
    )(other, mine, act, der, weights)


def ff_grads(two_other, two_mine, feed_other, feed_mine, ggate, gup, hid):
    rows, model = two_other.shape
    unit = FF_UNIT
    width = 384

    def body(to_ref, tm_ref, fo_ref, fm_ref, gg_ref, gu_ref, hid_ref, out_ref):
        def pair(o_ref, m_ref, r_ref):
            return (mm(o_ref[...], r_ref[:rows, :], TN) + mm(m_ref[...], r_ref[rows:, :], TN)).astype(BF)

        out_ref[:, :unit] = pair(to_ref, tm_ref, gg_ref)
        out_ref[:, unit : 2 * unit] = pair(to_ref, tm_ref, gu_ref)
        out_ref[:, 2 * unit :] = pair(fo_ref, fm_ref, hid_ref)

    cols = pl.BlockSpec((rows, width), lambda i: (0, i))
    whole = pl.BlockSpec((2 * rows, unit), lambda i: (0, 0))
    return pl.pallas_call(
        body,
        grid=(model // width,),
        in_specs=[cols] * 4 + [whole] * 3,
        out_specs=pl.BlockSpec((width, 3 * unit), lambda i: (i, 0)),
        out_shape=jax.ShapeDtypeStruct((model, 3 * unit), BF),
        cost_estimate=pl.CostEstimate(
            flops=12 * rows * model * unit, bytes_accessed=20_000_000, transcendentals=0
        ),
        name="ff_grads",
    )(two_other, two_mine, feed_other, feed_mine, ggate, gup, hid)


def ff_spread(mine, peer, info, ff_width):
    unit = FF_UNIT
    local = mine.shape[1]

    def body(info_ref, m_ref, p_ref, *outs):
        for r in range(8):
            e = lax.rem(r // 2 + 4 - info_ref[1], 4)
            use_mine = info_ref[2] == r % 2
            skip = 8 * unit - ff_width if r == 7 else 0
            for m in range(3):
                lo = m * unit + skip
                span = slice(lo, (m + 1) * unit)
                piece = jnp.where(use_mine, m_ref[e, :, span], p_ref[e, :, span])
                outs[m][:, r * unit : r * unit + unit - skip] = piece.astype(F32)

    vmem = pl.BlockSpec(memory_space=pltpu.VMEM)
    return pl.pallas_call(
        body,
        in_specs=[pl.BlockSpec(memory_space=pltpu.SMEM), vmem, vmem],
        out_specs=[vmem] * 3,
        out_shape=[jax.ShapeDtypeStruct((local, ff_width), F32)] * 3,
        cost_estimate=pl.CostEstimate(flops=0, bytes_accessed=10_000_000, transcendentals=0),
        name="ff_spread",
    )(info, mine, peer)


def after(values, others):
    return lax.optimization_barrier((values, others))[0]


def per_device(
    inputs,
    lengths,
    q_weight,
    k_weight,
    v_weight,
    o_weight,
    gate_weight,
    up_weight,
    down_weight,
    attn_norm,
    attn_post_norm,
    mlp_norm,
    mlp_post_norm,
    query_norm,
    key_norm,
    cotangent,
):
    count, model = inputs.shape
    local = q_weight.shape[0]
    head_local = query_norm.shape[0]
    head_width = 16 * head_local
    q_width = q_weight.shape[1]
    q_half = q_width // 2
    ff_width = gate_weight.shape[1]
    heads = q_width // head_width
    scale = head_width ** (-0.5)
    rep = lax.axis_index("rep")
    shard = lax.axis_index("shard")
    zi, core = rep // 2, rep % 2
    xi, yi = shard // 4, shard % 4
    first = core == 0

    gain_cols = jnp.stack(
        [
            attn_norm,
            attn_post_norm,
            mlp_norm,
            mlp_post_norm,
            jnp.pad(jnp.concatenate([query_norm, key_norm]), (0, local - 2 * head_local)),
        ]
    )
    gain_cols = jnp.transpose(jnp.pad(gain_cols, ((0, 128 - gain_cols.shape[0]), (0, 0))))
    q_mine = lax.dynamic_slice_in_dim(q_weight, core * q_half, q_half, 1)
    o_mine = lax.dynamic_slice_in_dim(o_weight, core * q_half, q_half, 1)
    kv_mine = jnp.where(first, k_weight, v_weight)
    block_a = jnp.concatenate([q_mine, kv_mine], axis=1)
    block_b = jnp.concatenate([o_mine, gain_cols], axis=1)
    near_a = jnp.stack(direct_gather(block_a, "x"))
    near_b = jnp.stack(direct_gather(block_b, "y"))
    unit = FF_UNIT
    first_unit = jnp.minimum(rep * unit, ff_width - unit)
    info = jnp.stack([rep * unit - first_unit, zi, core, xi, yi]).astype(jnp.int32)
    own_q, own_kv = place_xy(direct_gather(near_a, "y"), info, True, q_half)
    own_o, gain_w = place_xy(direct_gather(near_b, "x"), info, False, q_half)
    peer_q, peer_kv, peer_o = swap_core(own_q), swap_core(own_kv), swap_core(own_o)
    full_k = jnp.where(first, own_kv, peer_kv)
    full_v = jnp.where(first, peer_kv, own_kv)

    all_gains = jnp.transpose(gain_w[:, :8]).astype(F32)
    gain_attn, gain_post, gain_mid, gain_last = [all_gains[i] for i in range(4)]
    head_gains = all_gains[4].reshape(16, local)
    gain_query = head_gains[:, :head_local].reshape(head_width)
    gain_key = head_gains[:, head_local : 2 * head_local].reshape(head_width)

    ff_w = jnp.concatenate(
        [
            lax.dynamic_slice_in_dim(w, first_unit, unit, 1)
            for w in (gate_weight, up_weight, down_weight)
        ],
        axis=1,
    )
    ff_w = lax.all_gather(after(ff_w, (near_a, near_b)), "shard", axis=0, tiled=True)

    segment, live, position, row_ids = layout(lengths[0], count)
    live_col = live.astype(jnp.float32)[:, None]
    cosine, sine = rotary_tables(position, head_width)
    same = (segment[:, None] == segment[None, :]) & (row_ids[None, :] <= row_ids[:, None])
    residual = inputs.astype(F32)
    cot = cotangent.astype(F32)
    normed_one = norm_scale(residual, gain_attn).astype(BF)
    query_acc = jnp.concatenate(
        [
            jnp.dot(normed_one, own_q, preferred_element_type=F32),
            jnp.dot(normed_one, peer_q, preferred_element_type=F32),
        ],
        axis=1,
    )
    key_acc = jnp.dot(normed_one, full_k, preferred_element_type=F32)
    value_b = jnp.dot(normed_one, full_v, preferred_element_type=F32).astype(BF)
    query_heads = query_acc.reshape(count, heads, head_width)
    key_heads = key_acc.reshape(count, 1, head_width)
    query_rot = head_prep(query_heads, gain_query, cosine, sine).astype(BF)
    key_rot = head_prep(key_heads, gain_key, cosine, sine)[:, 0].astype(BF)

    raw = jnp.einsum("qhd,kd->hqk", query_rot, key_rot, preferred_element_type=F32) * scale
    scores = jnp.where(same[None], raw, NEGATIVE)
    peak = jnp.max(scores, axis=-1, keepdims=True)
    log_total = peak + jnp.log(jnp.sum(jnp.exp(scores - peak), axis=-1, keepdims=True))
    probs = jnp.exp(scores - log_total)
    probs_b = probs.astype(BF)
    mixed = jnp.einsum("hqk,kd->qhd", probs_b, value_b, preferred_element_type=F32)
    mixed = mixed.reshape(count, q_width).astype(BF)
    attention = dot_rows(mixed[:, :q_half], own_o) + dot_rows(mixed[:, q_half:], peer_o)
    middle = residual + norm_scale(attention, gain_post)
    normed_two = norm_scale(middle, gain_mid).astype(BF)

    two_other, two_mine = gather_rep(normed_two)
    hid, act, der, feed_other, feed_mine = ff_forward(two_other, two_mine, ff_w, info)
    feed = reduce_rep(feed_other, feed_mine)
    outputs = ((middle + norm_scale(feed, gain_last)) * live_col).astype(BF)

    grad_out = cot * live_col
    unused, pull_last = jax.vjp(norm_scale, feed, gain_last)
    grad_feed, grad_last = pull_last(grad_out)
    fb_other, fb_mine = gather_rep(grad_feed.astype(BF))
    gate_b, up_b, back_other, back_mine = ff_backward(fb_other, fb_mine, act, der, ff_w)
    ff_part = ff_grads(two_other, two_mine, fb_other, fb_mine, gate_b, up_b, hid)
    grad_normed = reduce_rep(back_other, back_mine)
    ff_own = lax.psum_scatter(ff_part, "shard", scatter_dimension=0, tiled=True)

    unused, pull_mid = jax.vjp(norm_scale, middle, gain_mid)
    back_mid, grad_mid = pull_mid(grad_normed)
    grad_middle = grad_out + back_mid
    unused, pull_post = jax.vjp(norm_scale, attention, gain_post)
    grad_attention, grad_post = pull_post(grad_middle)
    attention_b = grad_attention.astype(BF)
    grad_mixed = jnp.concatenate(
        [
            jnp.dot(attention_b, own_o, preferred_element_type=F32).astype(BF),
            jnp.dot(attention_b, peer_o, preferred_element_type=F32).astype(BF),
        ],
        axis=1,
    )
    grad_mixed = grad_mixed.reshape(count, heads, head_width)
    grad_probs = jnp.einsum("qhd,kd->hqk", grad_mixed, value_b, preferred_element_type=F32)
    inner = jnp.sum(probs * grad_probs, axis=-1, keepdims=True)
    grad_scores = (probs * (grad_probs - inner) * scale).astype(BF)
    grad_qrot = jnp.einsum("hqk,kd->qhd", grad_scores, key_rot, preferred_element_type=F32)
    grad_krot = jnp.einsum("hqk,qhd->kd", grad_scores, query_rot, preferred_element_type=F32)
    grad_value = jnp.einsum("hqk,qhd->kd", probs_b, grad_mixed, preferred_element_type=F32)
    unused, pull_query = jax.vjp(
        lambda values, gain: head_prep(values, gain, cosine, sine), query_heads, gain_query
    )
    grad_query, grad_qgain = pull_query(grad_qrot)
    unused, pull_key = jax.vjp(
        lambda values, gain: head_prep(values, gain, cosine, sine), key_heads, gain_key
    )
    grad_key, grad_kgain = pull_key(grad_krot[:, None, :])
    query_b = grad_query.reshape(count, q_width).astype(BF)
    key_b = grad_key.reshape(count, head_width).astype(BF)
    value_grad_b = grad_value.astype(BF)
    grad_first_in = (
        dot_rows(query_b[:, :q_half], own_q)
        + dot_rows(query_b[:, q_half:], peer_q)
        + dot_rows(key_b, full_k)
        + dot_rows(value_grad_b, full_v)
    )
    unused, pull_first = jax.vjp(norm_scale, residual, gain_attn)
    back_first, grad_first = pull_first(grad_first_in)
    input_grad = (grad_middle + back_first).astype(BF)

    head_grads = jnp.pad(
        jnp.concatenate([grad_qgain.reshape(16, -1), grad_kgain.reshape(16, -1)], axis=1),
        ((0, 0), (0, local - 2 * head_local)),
    ).reshape(model)
    gain_grads = jnp.stack([grad_first, grad_post, grad_mid, grad_last, head_grads], axis=1)
    gain_grads = jnp.pad(gain_grads, ((0, 0), (0, 128 - gain_grads.shape[1]))).astype(BF)
    kv_keep = jnp.where(first, key_b, value_grad_b)
    kv_give = jnp.where(first, value_grad_b, key_b)
    keep_a = dot_cols(normed_one, jnp.concatenate([query_b[:, :q_half], kv_keep], axis=1))
    give_a = dot_cols(normed_one, jnp.concatenate([query_b[:, q_half:], kv_give], axis=1))
    keep_b = dot_cols(attention_b, mixed[:, :q_half])
    give_b = dot_cols(attention_b, mixed[:, q_half:])
    pair_a = (keep_a + swap_core(give_a.astype(BF)).astype(F32)).astype(BF)
    pair_b = (keep_b + swap_core(give_b.astype(BF)).astype(F32)).astype(BF)
    pair_g = (gain_grads.astype(F32) + swap_core(gain_grads).astype(F32)).astype(BF)
    pair_b = jnp.concatenate([pair_b, pair_g], axis=1)
    groups_a, groups_b = split_xy(pair_a, pair_b, xi, yi)
    first_a, first_b = direct_reduce(groups_a, "y"), direct_reduce(groups_b, "x")
    part_a, part_b = finish_xy(first_a, first_b, xi, yi)
    ff_own = after(ff_own, (part_a, part_b))
    ff_mine = jnp.stack(direct_gather(ff_own, "z"))
    pieces = ff_spread(ff_mine, swap_core(ff_mine), info, ff_width)
    part = jnp.concatenate([part_a, part_b], axis=1)
    part_s = part.astype(BF)
    total = part
    for d in (1, 2, 3):
        total = total + shift(part_s, "z", d).astype(F32)
    peer = swap_core(total.astype(BF)).astype(F32)
    low = jnp.where(first, total, peer)
    high = jnp.where(first, peer, total)
    kv = q_half + head_width
    gain_total = total[:, kv + q_half :]
    return (
        outputs,
        input_grad,
        jnp.concatenate([low[:, :q_half], high[:, :q_half]], axis=1),
        low[:, q_half:kv],
        high[:, q_half:kv],
        jnp.concatenate([low[:, kv : kv + q_half], high[:, kv : kv + q_half]], axis=1),
        pieces[0],
        pieces[1],
        pieces[2],
        gain_total[:, 0],
        gain_total[:, 1],
        gain_total[:, 2],
        gain_total[:, 3],
        gain_total[:head_local, 4],
        gain_total[head_local : 2 * head_local, 4],
    )


def solution(mesh):
    tokens, rows, vector = P(("rep", "shard"), None), P("shard", None), P("shard")
    in_specs = (tokens, tokens) + (rows,) * 7 + (vector,) * 6 + (tokens,)
    out_specs = (tokens, tokens) + (rows,) * 7 + (vector,) * 6
    return jax.shard_map(
        per_device, mesh=mesh, in_specs=in_specs, out_specs=out_specs, check_vma=False
    )
```

```python
import math

import jax
import jax.numpy as jnp
from jax import lax
from jax.experimental import pallas as pl
from jax.experimental.pallas import tpu as pltpu
from jax.sharding import PartitionSpec as P

EPSILON = 1e-06
NEGATIVE = -1e30
BF = jnp.bfloat16
F32 = jnp.float32


def norm_scale(values, gain):
    return values * lax.rsqrt(jnp.mean(values * values, axis=-1, keepdims=True) + EPSILON) * gain


def unit_rows(values):
    return values * lax.rsqrt(jnp.mean(values * values, axis=-1, keepdims=True) + EPSILON)


def layout(lengths, count):
    ends = jnp.cumsum(lengths)
    starts = ends - lengths
    row_ids = jnp.arange(count, dtype=jnp.int32)
    segment = jnp.sum((row_ids[:, None] >= ends[None, :]).astype(jnp.int32), axis=1)
    total = ends[-1]
    live = row_ids < total
    member = segment[:, None] == jnp.arange(lengths.shape[0], dtype=jnp.int32)[None, :]
    begin = jnp.sum(jnp.where(member, starts[None, :], 0), axis=1)
    begin = begin + jnp.where(live, 0, total)
    return (segment, live, row_ids - begin, row_ids)


def rotary_tables(position, width):
    half = width // 2
    freqs = 10000.0 ** (-2.0 * jnp.arange(half, dtype=jnp.float32) / width)
    angle = position.astype(jnp.float32)[:, None] * freqs[None, :]
    return (jnp.cos(angle), jnp.sin(angle))


def head_prep(values, gain, cosine, sine):
    normed = norm_scale(values, gain)
    half = values.shape[-1] // 2
    first = normed[..., :half]
    second = normed[..., half:]
    cos_b = cosine[:, None, :]
    sin_b = sine[:, None, :]
    return jnp.concatenate(
        [first * cos_b - second * sin_b, second * cos_b + first * sin_b], axis=-1
    )


def geglu(gate, up):
    return jax.nn.gelu(gate, approximate=True) * up


FF_UNIT = 896


def dot_rows(left, right):
    return lax.dot_general(
        left, right, (((1,), (1,)), ((), ())), preferred_element_type=jnp.float32
    )


def dot_cols(left, right):
    return lax.dot_general(
        left, right, (((0,), (0,)), ((), ())), preferred_element_type=jnp.float32
    )


def z_perm(d):
    return [(i, ((i // 2 + d) % 4) * 2 + i % 2) for i in range(8)]


CORE_PERM = [(i, i ^ 1) for i in range(8)]


def x_perm(d):
    return [(i, ((i // 4 + d) % 4) * 4 + i % 4) for i in range(16)]


def y_perm(d):
    return [(i, (i // 4) * 4 + (i % 4 + d) % 4) for i in range(16)]


def shift(v, axis, d):
    if axis == "z":
        return lax.ppermute(v, "rep", z_perm(d % 4))
    return lax.ppermute(v, "shard", x_perm(d % 4) if axis == "x" else y_perm(d % 4))


def swap_core(v):
    return lax.ppermute(v, "rep", CORE_PERM)


def direct_gather(own, axis):
    return [own] + [shift(own, axis, -e) for e in (1, 2, 3)]


def direct_reduce(groups, axis):
    total = groups[0].astype(F32)
    for e in (1, 2, 3):
        total = total + shift(groups[e], axis, e).astype(F32)
    return total


def pick(stack, index, axis, e):
    return lax.dynamic_index_in_dim(stack, (index + e) % 4, axis, keepdims=False)


def split_xy(one, two, xi, yi):
    rows = one.shape[0] // 16
    one = one.reshape(4, 4, rows, -1)
    two = two.reshape(4, 4, rows, -1)
    return [pick(one, yi, 1, e) for e in range(4)], [pick(two, xi, 0, e) for e in range(4)]


def finish_xy(one, two, xi, yi):
    one, two = one.astype(BF), two.astype(BF)
    one = direct_reduce([pick(one, xi, 0, e) for e in range(4)], "x")
    two = direct_reduce([pick(two, yi, 0, e) for e in range(4)], "y")
    return one, two


def place_xy(pieces, info, x_inside, split):
    rows, width = pieces[0].shape[1:]

    def body(info_ref, *refs):
        low_ref, high_ref = refs[4:]
        for e in range(4):
            for f in range(4):
                dx, dy = (f, e) if x_inside else (e, f)
                x = lax.rem(info_ref[3] + dx, 4)
                y = lax.rem(info_ref[4] + dy, 4)
                low_ref[x * 4 + y] = refs[e][f, :, :split]
                high_ref[x * 4 + y] = refs[e][f, :, split:]

    vmem = pl.BlockSpec(memory_space=pltpu.VMEM)
    low, high = pl.pallas_call(
        body,
        in_specs=[pl.BlockSpec(memory_space=pltpu.SMEM)] + [vmem] * 4,
        out_specs=[vmem, vmem],
        out_shape=[
            jax.ShapeDtypeStruct((16, rows, split), BF),
            jax.ShapeDtypeStruct((16, rows, width - split), BF),
        ],
        cost_estimate=pl.CostEstimate(flops=0, bytes_accessed=4_000_000, transcendentals=0),
        name="place_xy",
    )(info, *pieces)
    return low.reshape(16 * rows, split), high.reshape(16 * rows, width - split)


def gather_rep(v):
    mine = jnp.concatenate(direct_gather(v, "z"), axis=0)
    return swap_core(mine), mine


def reduce_rep(other, mine):
    total = mine.astype(F32) + swap_core(other).astype(F32)
    count = total.shape[0] // 4
    sends = total[count:].astype(BF)
    out = total[:count]
    for e in (1, 2, 3):
        out = out + shift(sends[(e - 1) * count : e * count], "z", e).astype(F32)
    return out


TILE = 256
CHUNKS = ((0, 896),)
NT = (((1,), (1,)), ((), ()))
TN = (((0,), (0,)), ((), ()))


def mm(left, right, dims=(((1,), (0,)), ((), ()))):
    return lax.dot_general(left, right, dims, preferred_element_type=F32)


def row_specs(width, steps):
    half = steps // 2
    return [
        pl.BlockSpec((TILE, width), lambda i: (jnp.minimum(i, half - 1), 0)),
        pl.BlockSpec((TILE, width), lambda i: (jnp.maximum(i - half, 0), 0)),
    ]


def put_rows(step, half, value, other_ref, mine_ref):
    @pl.when(step < half)
    def _():
        other_ref[...] = value.astype(other_ref.dtype)

    @pl.when(step >= half)
    def _():
        mine_ref[...] = value.astype(mine_ref.dtype)


def ff_forward(other, mine, weights, info):
    steps = 2 * other.shape[0] // TILE
    model, unit = other.shape[1], FF_UNIT
    half = steps // 2

    def body(info_ref, o_ref, m_ref, w_ref, hid_ref, act_ref, der_ref, fo_ref, fm_ref):
        step = pl.program_id(0)
        x = jnp.where(step < half, o_ref[...], m_ref[...])
        feed = 0.0
        c = math.sqrt(2.0 / math.pi)
        for lo, hi in CHUNKS:
            gate = mm(x, w_ref[:, lo:hi])
            up = mm(x, w_ref[:, unit + lo : unit + hi])
            col = lo + lax.broadcasted_iota(jnp.int32, gate.shape, 1)
            valid = col >= info_ref[0]
            square = gate * gate
            t = jnp.tanh(c * (gate + 0.044715 * (gate * square)))
            act = jnp.where(valid, 0.5 * gate * (1.0 + t), 0.0)
            slope = 0.5 * (1.0 + t) + 0.5 * gate * (1.0 - t * t) * (
                c + (3 * 0.044715 * c) * square
            )
            hid = (act * up).astype(BF)
            hid_ref[:, lo:hi] = hid
            act_ref[:, lo:hi] = act.astype(BF)
            der_ref[:, lo:hi] = jnp.where(valid, slope * up, 0.0).astype(BF)
            feed = feed + mm(hid, w_ref[:, 2 * unit + lo : 2 * unit + hi], NT)
        put_rows(step, half, feed, fo_ref, fm_ref)

    whole = lambda w: pl.BlockSpec(w.shape, lambda i: (0, 0))
    wide = pl.BlockSpec((TILE, unit), lambda i: (i, 0))
    rows = other.shape[0]
    return pl.pallas_call(
        body,
        grid=(steps,),
        in_specs=[pl.BlockSpec(memory_space=pltpu.SMEM)]
        + row_specs(model, steps)
        + [whole(weights)],
        out_specs=[wide, wide, wide] + row_specs(model, steps),
        out_shape=[jax.ShapeDtypeStruct((2 * rows, unit), BF)] * 3
        + [jax.ShapeDtypeStruct((rows, model), BF)] * 2,
        cost_estimate=pl.CostEstimate(
            flops=12 * rows * model * unit, bytes_accessed=20_000_000, transcendentals=0
        ),
        name="ff_forward",
    )(info, other, mine, weights)


def ff_backward(other, mine, act, der, weights):
    steps = 2 * other.shape[0] // TILE
    model, unit = other.shape[1], FF_UNIT
    half = steps // 2

    def body(o_ref, m_ref, act_ref, der_ref, w_ref, gg_ref, gu_ref, bo_ref, bm_ref):
        step = pl.program_id(0)
        x = jnp.where(step < half, o_ref[...], m_ref[...])
        back = 0.0
        for lo, hi in CHUNKS:
            ghid = mm(x, w_ref[:, 2 * unit + lo : 2 * unit + hi])
            ggate = (ghid * der_ref[:, lo:hi].astype(F32)).astype(BF)
            gup = (ghid * act_ref[:, lo:hi].astype(F32)).astype(BF)
            gg_ref[:, lo:hi] = ggate
            gu_ref[:, lo:hi] = gup
            back = back + mm(ggate, w_ref[:, lo:hi], NT)
            back = back + mm(gup, w_ref[:, unit + lo : unit + hi], NT)
        put_rows(step, half, back, bo_ref, bm_ref)

    whole = lambda w: pl.BlockSpec(w.shape, lambda i: (0, 0))
    wide = pl.BlockSpec((TILE, unit), lambda i: (i, 0))
    rows = other.shape[0]
    return pl.pallas_call(
        body,
        grid=(steps,),
        in_specs=row_specs(model, steps) + [wide, wide, whole(weights)],
        out_specs=[wide, wide] + row_specs(model, steps),
        out_shape=[jax.ShapeDtypeStruct((2 * rows, unit), BF)] * 2
        + [jax.ShapeDtypeStruct((rows, model), BF)] * 2,
        cost_estimate=pl.CostEstimate(
            flops=12 * rows * model * unit, bytes_accessed=20_000_000, transcendentals=0
        ),
        name="ff_backward",
    )(other, mine, act, der, weights)


def ff_grads(two_other, two_mine, feed_other, feed_mine, ggate, gup, hid):
    rows, model = two_other.shape
    unit = FF_UNIT
    width = 384

    def body(to_ref, tm_ref, fo_ref, fm_ref, gg_ref, gu_ref, hid_ref, out_ref):
        def pair(o_ref, m_ref, r_ref):
            return (mm(o_ref[...], r_ref[:rows, :], TN) + mm(m_ref[...], r_ref[rows:, :], TN)).astype(BF)

        out_ref[:, :unit] = pair(to_ref, tm_ref, gg_ref)
        out_ref[:, unit : 2 * unit] = pair(to_ref, tm_ref, gu_ref)
        out_ref[:, 2 * unit :] = pair(fo_ref, fm_ref, hid_ref)

    cols = pl.BlockSpec((rows, width), lambda i: (0, i))
    whole = pl.BlockSpec((2 * rows, unit), lambda i: (0, 0))
    return pl.pallas_call(
        body,
        grid=(model // width,),
        in_specs=[cols] * 4 + [whole] * 3,
        out_specs=pl.BlockSpec((width, 3 * unit), lambda i: (i, 0)),
        out_shape=jax.ShapeDtypeStruct((model, 3 * unit), BF),
        cost_estimate=pl.CostEstimate(
            flops=12 * rows * model * unit, bytes_accessed=20_000_000, transcendentals=0
        ),
        name="ff_grads",
    )(two_other, two_mine, feed_other, feed_mine, ggate, gup, hid)


def ff_spread(mine, peer, info, ff_width):
    unit = FF_UNIT
    local = mine.shape[1]

    def body(info_ref, m_ref, p_ref, *outs):
        for r in range(8):
            e = lax.rem(r // 2 + 4 - info_ref[1], 4)
            use_mine = info_ref[2] == r % 2
            skip = 8 * unit - ff_width if r == 7 else 0
            for m in range(3):
                lo = m * unit + skip
                span = slice(lo, (m + 1) * unit)
                piece = jnp.where(use_mine, m_ref[e, :, span], p_ref[e, :, span])
                outs[m][:, r * unit : r * unit + unit - skip] = piece.astype(F32)

    vmem = pl.BlockSpec(memory_space=pltpu.VMEM)
    return pl.pallas_call(
        body,
        in_specs=[pl.BlockSpec(memory_space=pltpu.SMEM), vmem, vmem],
        out_specs=[vmem] * 3,
        out_shape=[jax.ShapeDtypeStruct((local, ff_width), F32)] * 3,
        cost_estimate=pl.CostEstimate(flops=0, bytes_accessed=10_000_000, transcendentals=0),
        name="ff_spread",
    )(info, mine, peer)


def after(values, others):
    return lax.optimization_barrier((values, others))[0]


def per_device(
    inputs,
    lengths,
    q_weight,
    k_weight,
    v_weight,
    o_weight,
    gate_weight,
    up_weight,
    down_weight,
    attn_norm,
    attn_post_norm,
    mlp_norm,
    mlp_post_norm,
    query_norm,
    key_norm,
    cotangent,
):
    count, model = inputs.shape
    local = q_weight.shape[0]
    head_local = query_norm.shape[0]
    head_width = 16 * head_local
    q_width = q_weight.shape[1]
    q_half = q_width // 2
    ff_width = gate_weight.shape[1]
    heads = q_width // head_width
    scale = head_width ** (-0.5)
    rep = lax.axis_index("rep")
    shard = lax.axis_index("shard")
    zi, core = rep // 2, rep % 2
    xi, yi = shard // 4, shard % 4
    first = core == 0

    gain_cols = jnp.stack(
        [
            attn_norm,
            attn_post_norm,
            mlp_norm,
            mlp_post_norm,
            jnp.pad(jnp.concatenate([query_norm, key_norm]), (0, local - 2 * head_local)),
        ]
    )
    gain_cols = jnp.transpose(jnp.pad(gain_cols, ((0, 128 - gain_cols.shape[0]), (0, 0))))
    q_mine = lax.dynamic_slice_in_dim(q_weight, core * q_half, q_half, 1)
    o_mine = lax.dynamic_slice_in_dim(o_weight, core * q_half, q_half, 1)
    kv_mine = jnp.where(first, k_weight, v_weight)
    block_a = jnp.concatenate([q_mine, kv_mine], axis=1)
    block_b = jnp.concatenate([o_mine, gain_cols], axis=1)
    near_a = jnp.stack(direct_gather(block_a, "x"))
    near_b = jnp.stack(direct_gather(block_b, "y"))
    unit = FF_UNIT
    first_unit = jnp.minimum(rep * unit, ff_width - unit)
    info = jnp.stack([rep * unit - first_unit, zi, core, xi, yi]).astype(jnp.int32)
    own_q, own_kv = place_xy(direct_gather(near_a, "y"), info, True, q_half)
    own_o, gain_w = place_xy(direct_gather(near_b, "x"), info, False, q_half)
    peer_q, peer_kv, peer_o = swap_core(own_q), swap_core(own_kv), swap_core(own_o)
    full_k = jnp.where(first, own_kv, peer_kv)
    full_v = jnp.where(first, peer_kv, own_kv)

    all_gains = jnp.transpose(gain_w[:, :8]).astype(F32)
    gain_attn, gain_post, gain_mid, gain_last = [all_gains[i] for i in range(4)]
    head_gains = all_gains[4].reshape(16, local)
    gain_query = head_gains[:, :head_local].reshape(head_width)
    gain_key = head_gains[:, head_local : 2 * head_local].reshape(head_width)

    ff_w = jnp.concatenate(
        [
            lax.dynamic_slice_in_dim(w, first_unit, unit, 1)
            for w in (gate_weight, up_weight, down_weight)
        ],
        axis=1,
    )
    ff_w = lax.all_gather(after(ff_w, (near_a, near_b)), "shard", axis=0, tiled=True)

    segment, live, position, row_ids = layout(lengths[0], count)
    live_col = live.astype(jnp.float32)[:, None]
    cosine, sine = rotary_tables(position, head_width)
    same = (segment[:, None] == segment[None, :]) & (row_ids[None, :] <= row_ids[:, None])
    residual = inputs.astype(F32)
    cot = cotangent.astype(F32)
    normed_one = norm_scale(residual, gain_attn).astype(BF)
    query_acc = jnp.concatenate(
        [
            jnp.dot(normed_one, own_q, preferred_element_type=F32),
            jnp.dot(normed_one, peer_q, preferred_element_type=F32),
        ],
        axis=1,
    )
    key_acc = jnp.dot(normed_one, full_k, preferred_element_type=F32)
    value_b = jnp.dot(normed_one, full_v, preferred_element_type=F32).astype(BF)
    query_heads = query_acc.reshape(count, heads, head_width)
    key_heads = key_acc.reshape(count, 1, head_width)
    query_rot = head_prep(query_heads, gain_query, cosine, sine).astype(BF)
    key_rot = head_prep(key_heads, gain_key, cosine, sine)[:, 0].astype(BF)

    raw = jnp.einsum("qhd,kd->hqk", query_rot, key_rot, preferred_element_type=F32) * scale
    scores = jnp.where(same[None], raw, NEGATIVE)
    peak = jnp.max(scores, axis=-1, keepdims=True)
    log_total = peak + jnp.log(jnp.sum(jnp.exp(scores - peak), axis=-1, keepdims=True))
    probs = jnp.exp(scores - log_total)
    probs_b = probs.astype(BF)
    mixed = jnp.einsum("hqk,kd->qhd", probs_b, value_b, preferred_element_type=F32)
    mixed = mixed.reshape(count, q_width).astype(BF)
    attention = dot_rows(mixed[:, :q_half], own_o) + dot_rows(mixed[:, q_half:], peer_o)
    middle = residual + norm_scale(attention, gain_post)
    normed_two = norm_scale(middle, gain_mid).astype(BF)

    two_other, two_mine = gather_rep(normed_two)
    hid, act, der, feed_other, feed_mine = ff_forward(two_other, two_mine, ff_w, info)
    feed = reduce_rep(feed_other, feed_mine)
    outputs = ((middle + norm_scale(feed, gain_last)) * live_col).astype(BF)

    grad_out = cot * live_col
    unused, pull_last = jax.vjp(norm_scale, feed, gain_last)
    grad_feed, grad_last = pull_last(grad_out)
    fb_other, fb_mine = gather_rep(grad_feed.astype(BF))
    gate_b, up_b, back_other, back_mine = ff_backward(fb_other, fb_mine, act, der, ff_w)
    ff_part = ff_grads(two_other, two_mine, fb_other, fb_mine, gate_b, up_b, hid)
    grad_normed = reduce_rep(back_other, back_mine)
    ff_own = lax.psum_scatter(ff_part, "shard", scatter_dimension=0, tiled=True)

    unused, pull_mid = jax.vjp(norm_scale, middle, gain_mid)
    back_mid, grad_mid = pull_mid(grad_normed)
    grad_middle = grad_out + back_mid
    unused, pull_post = jax.vjp(norm_scale, attention, gain_post)
    grad_attention, grad_post = pull_post(grad_middle)
    attention_b = grad_attention.astype(BF)
    grad_mixed = jnp.concatenate(
        [
            jnp.dot(attention_b, own_o, preferred_element_type=F32).astype(BF),
            jnp.dot(attention_b, peer_o, preferred_element_type=F32).astype(BF),
        ],
        axis=1,
    )
    grad_mixed = grad_mixed.reshape(count, heads, head_width)
    grad_probs = jnp.einsum("qhd,kd->hqk", grad_mixed, value_b, preferred_element_type=F32)
    inner = jnp.sum(probs * grad_probs, axis=-1, keepdims=True)
    grad_scores = (probs * (grad_probs - inner) * scale).astype(BF)
    grad_qrot = jnp.einsum("hqk,kd->qhd", grad_scores, key_rot, preferred_element_type=F32)
    grad_krot = jnp.einsum("hqk,qhd->kd", grad_scores, query_rot, preferred_element_type=F32)
    grad_value = jnp.einsum("hqk,qhd->kd", probs_b, grad_mixed, preferred_element_type=F32)
    unused, pull_query = jax.vjp(
        lambda values, gain: head_prep(values, gain, cosine, sine), query_heads, gain_query
    )
    grad_query, grad_qgain = pull_query(grad_qrot)
    unused, pull_key = jax.vjp(
        lambda values, gain: head_prep(values, gain, cosine, sine), key_heads, gain_key
    )
    grad_key, grad_kgain = pull_key(grad_krot[:, None, :])
    query_b = grad_query.reshape(count, q_width).astype(BF)
    key_b = grad_key.reshape(count, head_width).astype(BF)
    value_grad_b = grad_value.astype(BF)
    grad_first_in = (
        dot_rows(query_b[:, :q_half], own_q)
        + dot_rows(query_b[:, q_half:], peer_q)
        + dot_rows(key_b, full_k)
        + dot_rows(value_grad_b, full_v)
    )
    unused, pull_first = jax.vjp(norm_scale, residual, gain_attn)
    back_first, grad_first = pull_first(grad_first_in)
    input_grad = (grad_middle + back_first).astype(BF)

    head_grads = jnp.pad(
        jnp.concatenate([grad_qgain.reshape(16, -1), grad_kgain.reshape(16, -1)], axis=1),
        ((0, 0), (0, local - 2 * head_local)),
    ).reshape(model)
    gain_grads = jnp.stack([grad_first, grad_post, grad_mid, grad_last, head_grads], axis=1)
    gain_grads = jnp.pad(gain_grads, ((0, 0), (0, 128 - gain_grads.shape[1]))).astype(BF)
    kv_keep = jnp.where(first, key_b, value_grad_b)
    kv_give = jnp.where(first, value_grad_b, key_b)
    keep_a = dot_cols(normed_one, jnp.concatenate([query_b[:, :q_half], kv_keep], axis=1))
    give_a = dot_cols(normed_one, jnp.concatenate([query_b[:, q_half:], kv_give], axis=1))
    keep_b = dot_cols(attention_b, mixed[:, :q_half])
    give_b = dot_cols(attention_b, mixed[:, q_half:])
    pair_a = (keep_a + swap_core(give_a.astype(BF)).astype(F32)).astype(BF)
    pair_b = (keep_b + swap_core(give_b.astype(BF)).astype(F32)).astype(BF)
    pair_g = (gain_grads.astype(F32) + swap_core(gain_grads).astype(F32)).astype(BF)
    pair_b = jnp.concatenate([pair_b, pair_g], axis=1)
    groups_a, groups_b = split_xy(pair_a, pair_b, xi, yi)
    first_a, first_b = direct_reduce(groups_a, "y"), direct_reduce(groups_b, "x")
    ff_own = after(ff_own, (first_a, first_b))
    ff_mine = jnp.stack(direct_gather(ff_own, "z"))
    pieces = ff_spread(ff_mine, swap_core(ff_mine), info, ff_width)
    part_a, part_b = finish_xy(first_a, first_b, xi, yi)
    part = jnp.concatenate([part_a, part_b], axis=1)
    part_s = part.astype(BF)
    total = part
    for d in (1, 2, 3):
        total = total + shift(part_s, "z", d).astype(F32)
    peer = swap_core(total.astype(BF)).astype(F32)
    low = jnp.where(first, total, peer)
    high = jnp.where(first, peer, total)
    kv = q_half + head_width
    gain_total = total[:, kv + q_half :]
    return (
        outputs,
        input_grad,
        jnp.concatenate([low[:, :q_half], high[:, :q_half]], axis=1),
        low[:, q_half:kv],
        high[:, q_half:kv],
        jnp.concatenate([low[:, kv : kv + q_half], high[:, kv : kv + q_half]], axis=1),
        pieces[0],
        pieces[1],
        pieces[2],
        gain_total[:, 0],
        gain_total[:, 1],
        gain_total[:, 2],
        gain_total[:, 3],
        gain_total[:head_local, 4],
        gain_total[head_local : 2 * head_local, 4],
    )


def solution(mesh):
    tokens, rows, vector = P(("rep", "shard"), None), P("shard", None), P("shard")
    in_specs = (tokens, tokens) + (rows,) * 7 + (vector,) * 6 + (tokens,)
    out_specs = (tokens, tokens) + (rows,) * 7 + (vector,) * 6
    return jax.shard_map(
        per_device, mesh=mesh, in_specs=in_specs, out_specs=out_specs, check_vma=False
    )
```
